512 devices in a mesh: ctx: 64 (over x_lo, z, core), tp: 8 (over y, x_hi).
Axes of the slice: x: 4 (x_hi: 2, x_lo: 2; x = x_hi * 2 + x_lo), y: 4, z: 16, core: 2. Of those that a mesh axis runs over, the one named last changes fastest.
Arguments:
- projected: bfloat16 [24576, 3, 8192], P('ctx', None, 'tp'), may hold values from -6 to 6
- dest_shard: int32 [24576], P('ctx'), may hold values from 0 to 63, as said below
- seg_start: int32 [24576], P('ctx'), may hold values from 0 to 24575, as said below
- short_filter: bfloat16 [7, 3, 8192], P(None, None, 'tp'), may hold values from -2 to 2
- long_filter: bfloat16 [128, 512], P(None, 'tp'), may hold values from -0.75 to 0.75
- long_decay: float32 [512], P('tp'), may hold values from 0.001953125 to 0.03125
- out_proj: bfloat16 [4096, 8192], P('ctx', 'tp'), may hold values from -0.0625 to 0.0625
Outputs:
- block_out: bfloat16 [24576, 4096], P('ctx', 'tp')
The draws below stay inside these ranges and needn't reach their ends.
Inputs may be any that keep to these rules, and one draw needn't show every extreme that they name: `dest_shard`: every context shard is named by exactly 384 rows in all. In each aligned block of 384 rows (the rows of one loader shard) a shard is named by at most 12 rows, and the rows naming one shard are consecutive; every block names some shard exactly 12 times, and every shard is named exactly 12 times by some block. `seg_start`: Non-decreasing, at most the position itself, equal to the position where a genome begins; positions with equal values form one genome. The last packed position begins a genome of its own.
All inputs are finite; a program needn't handle non-finite values.
Results may differ from the reference program's by a relative error of at most 0.012.
Values may be sent and summed in bfloat16 or wider, within the bound.
A program may use at most 128 MiB of HBM per device.

```python
import math
import jax
import jax.numpy as jnp
from jax import lax

D = 8192
DOUT = 4096
GROUP_CH = 16
SHORT = 7
MR_TAPS = 128
TOK_DEV = 384
TOKENS = 24576
FILTERS = 512
N_CTX = 64
N_TP = 8


def draw_dest_shard(key, part):
    shards = N_CTX
    half_cap = TOK_DEV // N_CTX
    subkeys = jax.random.split(key, 4)
    heights = jax.random.randint(subkeys[0], (shards,), 0, half_cap + 1)
    heights = heights.at[0].set(half_cap).at[shards - 1].set(0)
    circulant = half_cap + heights - jnp.roll(heights, 1)
    dest_rank = jax.random.permutation(subkeys[1], shards)
    source_rank = jax.random.permutation(subkeys[2], shards)
    counts = circulant[(dest_rank[None, :] - source_rank[:, None]) % shards]
    orders = jax.vmap(lambda one_key: jax.random.permutation(one_key, shards))(jax.random.split(subkeys[3], shards))
    run_lens = jnp.take_along_axis(counts, orders, axis=1)
    run_ends = jnp.cumsum(run_lens, axis=1)
    positions = jnp.arange(TOK_DEV)
    run_index = jnp.sum((run_ends[:, None, :] <= positions[None, :, None]).astype(jnp.int32), axis=2)
    targets = jnp.take_along_axis(orders, run_index, axis=1)
    return targets.reshape(TOKENS).astype(jnp.int32)


def draw_seg_start(key, part):
    shortest = max(TOK_DEV // 8, 1)
    longest = 2 * TOK_DEV
    lengths = jax.random.randint(key, (TOKENS,), shortest, longest + 1)
    begins = jnp.cumsum(lengths) - lengths
    positions = jnp.arange(TOKENS)
    genome_index = jnp.searchsorted(begins, positions, side='right') - 1
    starts = begins[genome_index]
    last_pos = TOKENS - 1
    starts = jnp.where(positions == last_pos, last_pos, starts)
    return starts.astype(jnp.int32)


def levels(rng, shape, cuts, smallest, top_value):
    def one(dim, shards_of):
        steps = jax.random.uniform(jax.random.fold_in(jax.random.fold_in(rng, 6), dim), (shards_of,), jnp.float32, smallest / len(cuts), top_value / len(cuts))
        return jnp.repeat(jnp.exp(steps), shape[dim] // shards_of).reshape((-1,) + (1,) * (len(shape) - dim - 1))

    factor_of = one(*cuts[0])
    for cut in cuts[1:]:
        factor_of = factor_of * one(*cut)
    return factor_of


def centred(stream_key, shape, deviation, most, pieces=(), kind=jnp.bfloat16):
    drawn = deviation * jax.random.normal(stream_key, shape, jnp.float32)
    if pieces:
        drawn = drawn * levels(stream_key, shape, pieces, -0.22, 0.18)
    return jnp.clip(drawn, -most, most).astype(kind)


def setup_inputs(seed: int = 0) -> dict:
    seeds = jax.random.split(jax.random.key(seed), 8)
    return {
        "projected": centred(seeds[0], (TOKENS, 3, D), 1.0, 6.0, ((0, 64), (2, 8))),
        "dest_shard": draw_dest_shard(jax.random.fold_in(seeds[7], 71), 0),
        "seg_start": draw_seg_start(jax.random.fold_in(seeds[7], 71), 0),
        "short_filter": centred(seeds[3], (SHORT, 3, D), SHORT ** -0.5, 2.0, ((2, 8),)),
        "long_filter": centred(seeds[4], (MR_TAPS, FILTERS), (MR_TAPS // 2) ** -0.5, 0.75, ((1, 8),)),
        "long_decay": jnp.clip(jnp.exp(math.log(0.03125) - 2.7725887 * jax.random.uniform(seeds[5], (FILTERS,), jnp.float32) ** levels(seeds[5], (FILTERS,), ((0, 8),), -0.2, 0.2)), 0.001953125, 0.03125),
        "out_proj": centred(seeds[6], (DOUT, D), D ** -0.5, 0.0625, ((0, 64), (1, 8))),
    }


def reference(projected, dest_shard, seg_start, short_filter, long_filter, long_decay, out_proj):
    order_rows = jnp.argsort(dest_shard, stable=True)
    reach_rows = MR_TAPS + SHORT - 2
    offsets_mr = jnp.arange(MR_TAPS).astype(jnp.float32)
    tap_weights = (long_filter.astype(jnp.float32) * jnp.exp(-long_decay[None, :] * offsets_mr[:, None])).astype(jnp.bfloat16)
    channel_taps = jnp.repeat(tap_weights.astype(jnp.float32), GROUP_CH, axis=1)
    weights_all = out_proj.astype(jnp.float32).reshape(DOUT, N_TP, D // N_TP)
    short_taps = short_filter.astype(jnp.float32)

    def one_block(block_index):
        first_row = block_index * TOK_DEV
        global_rows = (first_row - reach_rows + jnp.arange(TOK_DEV + reach_rows)).astype(jnp.int32)
        inside = global_rows >= 0
        safe_rows = jnp.where(inside, global_rows, 0).astype(jnp.int32)
        window = jnp.where(inside[:, None, None], projected[order_rows[safe_rows]], jnp.zeros((), jnp.bfloat16))
        begins = seg_start[safe_rows]
        count_out = TOK_DEV + MR_TAPS - 1
        out_pos = global_rows[SHORT - 1:]
        out_begin = begins[SHORT - 1:]
        features = jnp.zeros((count_out, 3, D), jnp.float32)
        for offset in range(SHORT):
            allowed = out_pos - offset >= out_begin
            product = short_taps[offset] * window[SHORT - 1 - offset: SHORT - 1 - offset + count_out].astype(jnp.float32)
            features = features + jnp.where(allowed[:, None, None], product, jnp.float32(0.0))
        queries = features[MR_TAPS - 1:, 0]
        key_value = (features[:, 1] * features[:, 2]).astype(jnp.bfloat16)
        local_pos = out_pos[MR_TAPS - 1:]
        local_begin = out_begin[MR_TAPS - 1:]

        def add_tap(offset, running):
            shifted = lax.dynamic_slice_in_dim(key_value, MR_TAPS - 1 - offset, TOK_DEV, 0).astype(jnp.float32)
            allowed = local_pos - offset >= local_begin
            return running + jnp.where(allowed[:, None], channel_taps[offset][None, :] * shifted, jnp.float32(0.0))

        mixing = lax.fori_loop(0, MR_TAPS, add_tap, jnp.zeros((TOK_DEV, D), jnp.float32))
        gated_out = (queries * mixing).astype(jnp.bfloat16)
        partials = jnp.einsum("tkc,okc->kto", gated_out.astype(jnp.float32).reshape(TOK_DEV, N_TP, D // N_TP), weights_all)
        rounded = lax.optimization_barrier(partials.astype(jnp.bfloat16))
        return jnp.sum(rounded.astype(jnp.float32), axis=0).astype(jnp.bfloat16)

    outputs = lax.map(one_block, jnp.arange(N_CTX))
    return outputs.reshape(TOKENS, DOUT)
```

```python
import functools

import jax
import jax.numpy as jnp
import numpy as np
from jax import lax
from jax.experimental import pallas as pl
from jax.experimental.pallas import tpu as pltpu
from jax.sharding import PartitionSpec as P

MESH = pl.DeviceIdType.MESH
BF = jnp.bfloat16
F32 = jnp.float32
I32 = jnp.int32

NZ = 16
NS = 4 * NZ
TOK = 384
CH = 1024
G = 4
CG = CH // G
W = 3 * CG
HALF = NZ // 2
PAIR = 12
HALO = 144
WORST = tuple(PAIR * (4 * (HALF - k) + 2) for k in range(1, HALF + 1))
LIMIT = 60 * 1024 * 1024


def up16(n):
    return -(-n // 16) * 16


def class_keys():
    d = np.arange(NS)
    zd, cd = (d // 2) % NZ, d % 2
    off = (zd[None, :] - np.arange(NZ)[:, None]) % NZ
    plus = (off > 0) & ((off < HALF) | ((off == HALF) & (cd[None, :] == 0)))
    kappa = np.where(off == 0, HALF, np.where(plus, HALF - off, HALF + NZ - off))
    return (kappa * NS + d[None, :]).astype(np.int32)


def column_starts(caps):
    total = sum(caps)
    offs = np.concatenate([[0], np.cumsum(caps)[:-1]])
    table = np.zeros((2, NZ), np.int32)
    for cm in range(2):
        for delta in range(1, NZ):
            if delta < HALF or (delta == HALF and cm == 0):
                table[cm, delta] = TOK + offs[delta - 1]
            else:
                k = NZ - delta
                table[cm, delta] = TOK + total + offs[k - 1] - (TOK - caps[k - 1])
    return table


def sort_kernel(pos_ref, proj_ref, out_ref):
    rows = lax.broadcasted_iota(I32, (TOK, TOK), 0)
    perm = (rows == pos_ref[...]).astype(F32).astype(BF)
    for i in range(3):
        out_ref[0, :, i * CG : (i + 1) * CG] = jnp.dot(
            perm, proj_ref[i], preferred_element_type=F32
        ).astype(BF)


def sort_rows(pos, proj):
    return pl.pallas_call(
        sort_kernel,
        grid=(G,),
        out_shape=jax.ShapeDtypeStruct((G, TOK, W), BF),
        in_specs=[
            pl.BlockSpec((1, TOK), lambda g: (0, 0)),
            pl.BlockSpec((3, TOK, CG), lambda g: (0, 0, g)),
        ],
        out_specs=pl.BlockSpec((1, TOK, W), lambda g: (g, 0, 0)),
        name="sort_rows",
    )(pos, proj)


def dispatch_kernel(
    caps,
    capm,
    sorted_ref,
    idx_ref,
    fin_ref,
    packed_ref,
    halo_ref,
    held,
    select,
    place,
    outgo,
    income,
    z_send,
    z_recv,
    m_send,
    m_recv,
    h_send,
    h_recv,
    own_sem,
):
    me = lax.axis_index("ctx")
    core = me % 2
    z = (me // 2) % NZ
    x = me // (2 * NZ)

    def at(xx, zz, cc):
        return {"ctx": (xx * NZ + zz) * 2 + cc}

    up, down = at(x, (z + 1) % NZ, core), at(x, (z + NZ - 1) % NZ, core)
    mates = [None, at(x, z, 1 - core), at(1 - x, z, core), at(1 - x, z, 1 - core)]
    after, before = {"ctx": (me + 1) % NS}, {"ctx": (me + NS - 1) % NS}

    barrier = pltpu.get_barrier_semaphore()
    greeted = [up, down] + mates[1:] + [after, before]
    for other in greeted:
        pl.semaphore_signal(barrier, inc=1, device_id=other, device_id_type=MESH)

    total = sum(caps)
    offs = [0]
    for cap in caps:
        offs.append(offs[-1] + cap)

    def own(g):
        return pltpu.make_async_copy(
            sorted_ref.at[g], held.at[g, pl.ds(0, TOK)], own_sem.at[g]
        )

    for g in range(G):
        own(g).start()

    pl.semaphore_wait(barrier, len(greeted))

    def hop(way, g, k):
        cap = caps[k - 1]
        if k == 1:
            src = sorted_ref.at[g, pl.ds(0 if way == 0 else TOK - cap, cap)]
        else:
            first = TOK + way * total + offs[k - 2]
            if way == 1:
                first = first + caps[k - 2] - cap
            src = held.at[g, pl.ds(first, cap)]
        return pltpu.make_async_remote_copy(
            src_ref=src,
            dst_ref=held.at[g, pl.ds(TOK + way * total + offs[k - 1], cap)],
            send_sem=z_send.at[way, g, k - 1],
            recv_sem=z_recv.at[way, g, k - 1],
            device_id=up if way == 0 else down,
            device_id_type=MESH,
        )

    def to_mate(g, r):
        return pltpu.make_async_remote_copy(
            src_ref=outgo.at[g, r - 1],
            dst_ref=income.at[g, pl.ds(r * capm, capm)],
            send_sem=m_send.at[g, r - 1],
            recv_sem=m_recv.at[g, r - 1],
            device_id=mates[r],
            device_id_type=MESH,
        )

    def to_next(g):
        return pltpu.make_async_remote_copy(
            src_ref=packed_ref.at[g, pl.ds(TOK - HALO, HALO)],
            dst_ref=halo_ref.at[g],
            send_sem=h_send.at[g],
            recv_sem=h_recv.at[g],
            device_id=after,
            device_id_type=MESH,
        )

    width = TOK + 2 * total

    def first_hops(g):
        for way in range(2):
            hop(way, g, 1).start()

    first_hops(0)
    for r in range(4):
        cols = lax.broadcasted_iota(I32, (capm, width), 1)
        select[r] = (cols == idx_ref[r]).astype(F32).astype(BF)
    cols = lax.broadcasted_iota(I32, (TOK, 4 * capm), 1)
    place[...] = (cols == fin_ref[...]).astype(F32).astype(BF)
    for g in range(G):
        own(g).wait()

    @pl.when(me == 0)
    def _():
        halo_ref[...] = jnp.zeros_like(halo_ref)

    order = (3, 2, 1, 0)

    def turn(t, carry):
        for j in range(4):

            @pl.when((t >= 1) & (t <= G))
            def _():
                for way in range(2):
                    hop(way, t - 1, j + 4).wait_recv()
                    hop(way, t - 1, j + 5).start()

            if j > 0:

                @pl.when(t < G)
                def _():
                    for way in range(2):
                        hop(way, t, j).wait_recv()
                        hop(way, t, j + 1).start()

            else:

                @pl.when((t >= 1) & (t < G))
                def _():
                    first_hops(t)

            @pl.when((t >= 2) & (t < G + 2))
            def _():
                g = t - 2
                if j == 0:
                    for way in range(2):
                        hop(way, g, 8).wait_recv()
                r = order[j]

                def tile(n, c):
                    lanes = pl.ds(pl.multiple_of(n * CG, CG), CG)
                    got = jnp.dot(
                        select[r], held[g, :, lanes], preferred_element_type=F32
                    ).astype(BF)
                    if r == 0:
                        income[g, 0:capm, lanes] = got
                    else:
                        outgo[g, r - 1, :, lanes] = got
                    return c

                lax.fori_loop(0, 3, tile, 0)
                if r > 0:
                    to_mate(g, r).start()

            if j == 1:

                @pl.when(t >= 3)
                def _():
                    g = t - 3
                    for r in range(1, 4):
                        to_mate(g, r).wait_recv()

                    def tile(n, c):
                        lanes = pl.ds(pl.multiple_of(n * CG, CG), CG)
                        packed_ref[g, :, lanes] = jnp.dot(
                            place[...], income[g, :, lanes], preferred_element_type=F32
                        ).astype(BF)
                        return c

                    lax.fori_loop(0, 3, tile, 0)

                    @pl.when(me < NS - 1)
                    def _():
                        to_next(g).start()

        return carry

    lax.fori_loop(0, G + 3, turn, 0)

    def finish(g, carry):
        for way in range(2):
            for k in range(1, HALF + 1):
                hop(way, g, k).wait_send()
        for r in range(1, 4):
            to_mate(g, r).wait_send()

        @pl.when(me < NS - 1)
        def _():
            to_next(g).wait_send()

        @pl.when(me > 0)
        def _():
            to_next(g).wait_recv()

        return carry

    lax.fori_loop(0, G, finish, 0)


def dispatch(caps, capm, collective, rows, idx, fin):
    width = TOK + 2 * sum(caps)
    vmem = pl.BlockSpec(memory_space=pltpu.VMEM)
    dma = pltpu.SemaphoreType.DMA
    return pl.pallas_call(
        functools.partial(dispatch_kernel, caps, capm),
        out_shape=(
            jax.ShapeDtypeStruct((G, TOK, W), BF),
            jax.ShapeDtypeStruct((G, HALO, W), BF),
        ),
        in_specs=[vmem] * 3,
        out_specs=(vmem, vmem),
        scratch_shapes=[
            pltpu.VMEM((G, width, W), BF),
            pltpu.VMEM((4, capm, width), BF),
            pltpu.VMEM((TOK, 4 * capm), BF),
            pltpu.VMEM((G, 3, capm, W), BF),
            pltpu.VMEM((G, 4 * capm, W), BF),
            dma((2, G, HALF)),
            dma((2, G, HALF)),
            dma((G, 3)),
            dma((G, 3)),
            dma((G,)),
            dma((G,)),
            dma((G,)),
        ],
        compiler_params=pltpu.CompilerParams(
            collective_id=collective, has_side_effects=True, vmem_limit_bytes=LIMIT
        ),
        name="dispatch",
    )(rows, idx, fin)


def filter_kernel(begin_ref, short_ref, long_ref, decay_ref, rows_ref, halo_ref, out_ref, ext, feat, kv, toep):
    shape = short_ref.shape
    taps_n = 128
    ext[0:HALO] = halo_ref[0].astype(F32)
    ext[HALO : HALO + TOK] = rows_ref[0].astype(F32)
    begin = begin_ref[...]

    groups = CG // 16
    tap = lax.broadcasted_iota(I32, (1, taps_n), 1).astype(F32)
    taps = (long_ref[...].astype(F32) * jnp.exp(-decay_ref[...] * tap)).astype(BF)
    back = (
        lax.broadcasted_iota(I32, (taps_n, 2 * taps_n), 1)
        == taps_n - lax.broadcasted_iota(I32, (taps_n, 2 * taps_n), 0)
    )
    turned = jnp.dot(taps, back.astype(F32).astype(BF), preferred_element_type=F32)

    block = 64
    for b in range(512 // block):
        first = b * block - 128
        local = lax.broadcasted_iota(I32, (block, 128), 0) + first
        if first < 0:
            start = jnp.broadcast_to(begin[0:1], (block, 128))
        else:
            start = jnp.broadcast_to(begin[first : first + block], (block, 128))
        age = local - start
        for n in range(CG // 128):
            made = []
            for i in range(3):
                if i == 0 and first < 0:
                    continue
                lanes = slice(i * CG + n * 128, i * CG + (n + 1) * 128)
                acc = None
                for j in range(shape[1]):
                    x = ext[HALO + first - j : HALO + first - j + block, lanes]
                    w = short_ref[i, j : j + 1, n * 128 : (n + 1) * 128].astype(F32)
                    term = jnp.where(age >= j, w * x, 0.0)
                    acc = term if acc is None else acc + term
                made.append(acc)
            kv[b * block : (b + 1) * block, n * 128 : (n + 1) * 128] = (
                made[-2] * made[-1]
            ).astype(BF)
            if first >= 0:
                feat[first : first + block, n * 128 : (n + 1) * 128] = made[0]

    for f in range(groups):
        band = jnp.broadcast_to(turned[f : f + 1], (128, 256))
        toep[f] = pltpu.roll(band, 0, 1, stride=1, stride_axis=0).astype(BF)
    lane_group = lax.broadcasted_iota(I32, (128, 128), 1) // 16
    for tb in range(TOK // 128):
        m = lax.broadcasted_iota(I32, (128, 256), 1) + (tb * 128 - 128)
        open_ = (m >= begin[tb * 128 : (tb + 1) * 128]).astype(F32).astype(BF)
        for n in range(CG // 128):
            cols = slice(n * 128, (n + 1) * 128)
            source = kv[tb * 128 : tb * 128 + 256, cols]
            mix = jnp.zeros((128, 128), F32)
            for f in range(8):
                part = jnp.dot(toep[n * 8 + f] * open_, source, preferred_element_type=F32)
                mix = jnp.where(lane_group == f, part, mix)
            out_ref[tb * 128 : (tb + 1) * 128, cols] = (
                feat[tb * 128 : (tb + 1) * 128, cols] * mix
            ).astype(BF)


def run_filters(begin, short, long_t, decay, rows, halo):
    groups = CG // 16
    return pl.pallas_call(
        filter_kernel,
        grid=(G,),
        out_shape=jax.ShapeDtypeStruct((TOK, CH), BF),
        in_specs=[
            pl.BlockSpec((TOK, 1), lambda g: (0, 0)),
            pl.BlockSpec((3, short.shape[1], CG), lambda g: (0, 0, g)),
            pl.BlockSpec((groups, 128), lambda g: (g, 0)),
            pl.BlockSpec((groups, 1), lambda g: (g, 0)),
            pl.BlockSpec((1, TOK, W), lambda g: (g, 0, 0)),
            pl.BlockSpec((1, HALO, W), lambda g: (g, 0, 0)),
        ],
        out_specs=pl.BlockSpec((TOK, CG), lambda g: (0, g)),
        scratch_shapes=[
            pltpu.VMEM((HALO + TOK, W), F32),
            pltpu.VMEM((TOK, CG), F32),
            pltpu.VMEM((512, CG), BF),
            pltpu.VMEM((groups, 128, 256), BF),
        ],
        name="filters",
    )(begin, short, long_t, decay, rows, halo)


def project_kernel(gated_ref, weight_ref, out_ref):
    out_ref[0] = lax.dot_general(
        gated_ref[...],
        weight_ref[...],
        (((1,), (1,)), ((), ())),
        preferred_element_type=F32,
    ).astype(BF)


def project(gated, weights, parts):
    wide = weights.shape[0] // parts
    return pl.pallas_call(
        project_kernel,
        grid=(parts,),
        out_shape=jax.ShapeDtypeStruct((parts, TOK, wide), BF),
        in_specs=[
            pl.BlockSpec((TOK, CH), lambda k: (0, 0)),
            pl.BlockSpec((wide, CH), lambda k: (k, 0)),
        ],
        out_specs=pl.BlockSpec((1, TOK, wide), lambda k: (k, 0, 0)),
        name="project",
    )(gated, weights)


def tables(dest, caps, capm):
    me = lax.axis_index("ctx")
    core, z, x = me % 2, (me // 2) % NZ, me // (2 * NZ)
    d = jnp.arange(NS)
    r = jnp.arange(TOK)
    hit = dest[:, None] == d[None, :]
    counts = jnp.sum(hit.astype(I32), axis=0)
    first = jnp.min(jnp.where(hit, r[:, None], TOK), axis=0)
    key = lax.dynamic_index_in_dim(jnp.asarray(class_keys()), z, 0, keepdims=False)
    base = jnp.sum(jnp.where(key[None, :] < key[:, None], counts[None, :], 0), axis=1)
    pos = r + jnp.sum(jnp.where(hit, (base - first)[None, :], 0), axis=1)
    table = lax.all_gather(jnp.concatenate([counts, base]), "ctx")
    return pos.astype(I32).reshape(1, TOK), table


def receive_tables(table, caps, capm):
    me = lax.axis_index("ctx")
    core, z, x = me % 2, (me // 2) % NZ, me // (2 * NZ)
    rel = jnp.arange(4)
    xm, cm = (x + rel // 2) % 2, (core + rel % 2) % 2
    dm = (xm * NZ + z) * 2 + cm
    column = table.reshape(2, NZ, 2, 2 * NS)
    column = lax.dynamic_index_in_dim(column, x, 0, keepdims=False)
    column = lax.dynamic_index_in_dim(column, core, 1, keepdims=False)
    pick = (dm[:, None] == jnp.arange(NS)[None, :]).astype(I32)
    cnt = jnp.sum(pick[:, None, :] * column[None, :, :NS], axis=2)
    base = jnp.sum(pick[:, None, :] * column[None, :, NS:], axis=2)
    zs = jnp.arange(NZ)
    delta = (z - zs) % NZ
    starts = jnp.asarray(column_starts(caps))
    by_delta = jnp.sum(
        jnp.where(delta[None, :, None] == zs[None, None, :], starts[:, None, :], 0), axis=2
    )
    start = jnp.where(cm[:, None] == 0, by_delta[0][None], by_delta[1][None]) + base
    lower = (zs[None, :] < zs[:, None]).astype(I32)
    cum = jnp.sum(cnt[:, None, :] * lower[None], axis=2)
    i = jnp.arange(capm)[None, :, None]
    live = (i >= cum[:, None, :]) & (i < (cum + cnt)[:, None, :])
    idx = jnp.sum(jnp.where(live, (start - cum)[:, None, :] + i + 1, 0), axis=2) - 1
    mine = jnp.sum(
        jnp.where(jnp.arange(NS)[None, :] == me, table[:, :NS], 0), axis=1
    )
    s = jnp.arange(NS)
    xs, zz, cs = s // (2 * NZ), (s // 2) % NZ, s % 2
    at = jnp.sum(jnp.where(s[None, :] < s[:, None], mine[None, :], 0), axis=1)
    same = (xs[None, :] == xs[:, None]) & (cs[None, :] == cs[:, None]) & (zz[None, :] < zz[:, None])
    within = jnp.sum(jnp.where(same, mine[None, :], 0), axis=1)
    rank = ((xs + x) % 2) * 2 + (cs + core) % 2
    p = jnp.arange(TOK)[:, None]
    live = (p >= at[None, :]) & (p < (at + mine)[None, :])
    fin = jnp.sum(jnp.where(live, (rank * capm + within - at)[None, :] + p, 0), axis=1)
    return idx.astype(I32).reshape(4, capm, 1), fin.astype(I32).reshape(TOK, 1)


def body(projected, dest_shard, seg_start, short_filter, long_filter, long_decay, out_proj):
    me = lax.axis_index("ctx")
    proj = jnp.transpose(projected, (1, 0, 2))
    caps = tuple(up16(c) for c in WORST)
    capm = PAIR * NZ
    pos, table = tables(dest_shard, caps, capm)
    rows = sort_rows(pos, proj)
    idx, fin = receive_tables(table, caps, capm)
    packed, halo = dispatch(caps, capm, 0, rows, idx, fin)
    begin = (seg_start - me * TOK).astype(I32).reshape(TOK, 1)
    gated = run_filters(
        begin,
        jnp.transpose(short_filter, (1, 0, 2)),
        jnp.transpose(long_filter, (1, 0)),
        long_decay.reshape(-1, 1),
        packed,
        halo,
    )
    weights = lax.all_gather(out_proj, "ctx", tiled=True)
    part = project(gated, weights, lax.axis_size("tp"))
    got = lax.all_to_all(part, "tp", 0, 0, tiled=True)
    return jnp.sum(got.astype(F32), axis=0).astype(BF)


def solution(mesh):
    placed = (
        P("ctx", None, "tp"),
        P("ctx"),
        P("ctx"),
        P(None, None, "tp"),
        P(None, "tp"),
        P("tp"),
        P("ctx", "tp"),
    )
    return jax.shard_map(
        body, mesh=mesh, in_specs=placed, out_specs=P("ctx", "tp"), check_vma=False
    )
```
